512 devices in a mesh: ty: 16 (over x_hi, y, core), tx: 32 (over z, x_lo).
Axes of the slice: x: 4 (x_hi: 2, x_lo: 2; x = x_hi * 2 + x_lo), y: 4, z: 16, core: 2. Of those that a mesh axis runs over, the one named last changes fastest.
Arguments:
- incident: float32 [2, 5120, 12288], P(None, 'ty', 'tx'), may hold values from -6 to 6
- phases: float32 [2, 5120, 12288], P(None, 'ty', 'tx'), may hold values from -3.140625 to 3.140625
- cotangent: float32 [2, 5120, 12288], P(None, 'ty', 'tx'), may hold values from -6 to 6
- propagator: float32 [2, 33], replicated, may hold values from -0.6 to 0.6
Outputs:
- phase_grad: float32 [2, 5120, 12288], P(None, 'ty', 'tx')
- probe_grad: float32 [2, 5120, 12288], P(None, 'ty', 'tx')
The draws below stay inside these ranges and needn't reach their ends.
All inputs are finite; a program needn't handle non-finite values.
Results may differ from the reference program's by a relative error of at most 0.00015.
Values sent between devices are 32-bit elements; how exact they have to be, the bound alone decides.
No kernel may reach another device: no remote copies, remote signals or barrier semaphores. Data moves between devices by JAX's collectives and lax.ppermute only.
A program may use at most 64 MiB of HBM per device.

```python
import jax
import jax.numpy as jnp
from jax import lax

HY = 320
HX = 384
TAPS = 33
SLICES = 2
RIM = 16
NY = 5120
NX = 12288
N_TY = 16
N_TX = 32


def levels(own_key, extent, cuts, least, largest):
    level = 1.0
    for axis_at, blocks in cuts:
        heights = jax.random.uniform(jax.random.fold_in(jax.random.fold_in(own_key, 6), axis_at), (blocks,), jnp.float32, least / len(cuts), largest / len(cuts))
        level = level * jnp.repeat(jnp.exp(heights), extent[axis_at] // blocks).reshape((-1,) + (1,) * (len(extent) - 1 - axis_at))
    return level


def scatter_about(key, dims, width, bound, split=(), kind=jnp.bfloat16):
    result = jax.random.normal(key, dims, jnp.float32) * width
    if len(split) > 0:
        result = levels(key, dims, split, -0.22, 0.18) * result
    return jnp.clip(result, min=-bound, max=bound).astype(kind)


def setup_inputs(seed: int = 0) -> dict:
    key_of = jax.random.split(jax.random.key(seed), 5)
    return {
        "incident": scatter_about(key_of[0], (2, NY, NX), 1.0, 6.0, ((1, 16), (2, 32)), jnp.float32),
        "phases": jnp.clip(jax.random.uniform(key_of[1], (SLICES, NY, NX), jnp.float32, -3.140625, 3.140625), -3.140625, 3.140625),
        "cotangent": scatter_about(key_of[2], (2, NY, NX), 1.0, 6.0, ((1, 16), (2, 32)), jnp.float32),
        "propagator": scatter_about(key_of[3], (2, TAPS), 0.12, 0.6, (), jnp.float32),
    }


def spectrum(propagator, length):
    taps = lax.complex(propagator[0], propagator[1])
    places = (RIM - jnp.arange(TAPS, dtype=jnp.int32)) % length
    kernel = jnp.zeros((length,), taps.dtype).at[places].add(taps)
    return jnp.fft.fft(kernel)


def pass_rows(field, spec_rows):
    blocks = field.reshape(NY, N_TX, HX).transpose(1, 0, 2)

    def one_block(block):
        return jnp.fft.ifft(jnp.fft.fft(block, axis=0) * spec_rows[:, None], axis=0)

    return lax.map(one_block, blocks).transpose(1, 0, 2).reshape(NY, NX)


def pass_columns(field, spec_columns):
    blocks = field.reshape(N_TY, HY, NX)

    def one_block(block):
        return jnp.fft.ifft(jnp.fft.fft(block, axis=1) * spec_columns[None, :], axis=1)

    return lax.map(one_block, blocks).reshape(NY, NX)


def propagate(field, spec_rows, spec_columns):
    return pass_columns(pass_rows(field, spec_rows), spec_columns)


def phase_term(gradient, wavefield):
    return jnp.imag(gradient) * jnp.real(wavefield) - jnp.real(gradient) * jnp.imag(wavefield)


def reference(incident, phases, cotangent, propagator):
    spec_rows = spectrum(propagator, NY)
    spec_columns = spectrum(propagator, NX)
    adj_rows = jnp.conj(spec_rows)
    adj_columns = jnp.conj(spec_columns)
    trans_zero = lax.complex(jnp.cos(phases[0]), jnp.sin(phases[0]))
    trans_one = lax.complex(jnp.cos(phases[1]), jnp.sin(phases[1]))
    wave_zero = lax.complex(incident[0], incident[1]) * trans_zero
    wave_one = propagate(wave_zero, spec_rows, spec_columns) * trans_one
    grad_one = propagate(lax.complex(cotangent[0], cotangent[1]), adj_rows, adj_columns)
    grad_zero = propagate(grad_one * jnp.conj(trans_one), adj_rows, adj_columns)
    phase_grad = jnp.stack([phase_term(grad_zero, wave_zero), phase_term(grad_one, wave_one)])
    probe = grad_zero * jnp.conj(trans_zero)
    probe_grad = jnp.stack([jnp.real(probe), jnp.imag(probe)])
    return phase_grad, probe_grad
```

```python
import functools

import jax
import jax.numpy as jnp
from jax import lax
from jax.experimental import pallas as pl
from jax.experimental.pallas import tpu as pltpu
from jax.sharding import PartitionSpec as P

TAPS = 33
RIM = 16
HY = 320
HX = 384
EY = HY + 2 * RIM
BLOCK = 128
SPAN = BLOCK + 2 * RIM
PAD = 416
WIDE = 512
F32 = jnp.float32
BF16 = jnp.bfloat16

SIN = (0.9999999957265423, -0.1666665798726034, 0.008333051039472631, -0.0001980907830205207, 2.605240275509134e-06)
COS = (0.9999999997805725, -0.49999999358563046, 0.04166663626972161, -0.0013888361631194679, 2.4760176622410538e-05, -2.605181699425464e-07)

VM = pl.BlockSpec(memory_space=pltpu.VMEM)


def dot(a, b):
    return jnp.dot(a, b, preferred_element_type=F32)


def split(x):
    high = x.astype(BF16)
    return high, (x - high.astype(F32)).astype(BF16)


def cos_sin(phase):
    h = 0.5 * phase
    z = h * h
    s = jnp.full_like(z, SIN[-1])
    for k in SIN[-2::-1]:
        s = s * z + k
    s = s * h
    c = jnp.full_like(z, COS[-1])
    for k in COS[-2::-1]:
        c = c * z + k
    t = s + s
    return 1.0 - t * s, t * c


def edge_kernel(inc, ph, cot, up, down, ibuf, pbuf, sems):
    copies = []

    def copy(src, dst):
        c = pltpu.make_async_copy(src, dst, sems.at[len(copies)])
        c.start()
        copies.append(c)

    for side, out in enumerate((up, down)):
        near = pl.ds(HY - RIM, RIM) if side == 0 else pl.ds(0, RIM)
        far = pl.ds(HY - 2 * RIM, 2 * RIM) if side == 0 else pl.ds(0, 2 * RIM)
        copy(inc.at[:, near], ibuf.at[side])
        copy(ph.at[0, near], pbuf.at[side])
        copy(cot.at[0, far], out.at[pl.ds(32, 32)])
        copy(cot.at[1, far], out.at[pl.ds(64, 32)])
        copy(ph.at[1, near], out.at[pl.ds(96, 16)])
    for c in copies:
        c.wait()
    for side, out in enumerate((up, down)):
        c, s = cos_sin(pbuf[side])
        r, i = ibuf[side, 0], ibuf[side, 1]
        out[0:16] = r * c - i * s
        out[16:32] = r * s + i * c


def bands(row, size, shift):
    wide = jnp.broadcast_to(row, (size, 256))
    return pltpu.roll(wide, shift, 1, stride=1, stride_axis=0)


def local_kernel(taps, inc, ph, cot, m, t0, t1o, aa, wf, wa, cy, cxw, cxc, xh, xl, af):
    for adj, out in ((0, af), (1, aa)):
        sign = -1.0 if adj else 1.0
        br = bands(taps[2 * adj : 2 * adj + 1], BLOCK, 0)
        bi = sign * bands(taps[2 * adj + 1 : 2 * adj + 2], BLOCK, 0)
        full = jnp.concatenate([br, bi], 0)
        high, low = split(full)
        out[...] = jnp.concatenate([high[:, :SPAN], high[:, :SPAN], low[:, :SPAN]], 1)
        small = jnp.concatenate([br[:32], bi[:32]], 0)
        high, low = split(small)
        for side in range(2):
            at = slice(32 * side, 32 * side + 32)
            cy[2 * adj + side] = jnp.concatenate([high[:, at], high[:, at], low[:, at]], 1)
    for adj, out in ((0, wf), (1, wa)):
        sign = -1.0 if adj else 1.0
        wr = bands(taps[2 - 2 * adj : 3 - 2 * adj], SPAN, 256 - 32)[:, :BLOCK]
        wi = sign * bands(taps[3 - 2 * adj : 4 - 2 * adj], SPAN, 256 - 32)[:, :BLOCK]
        for k, w in enumerate((jnp.concatenate([wr, wi], 1), jnp.concatenate([-wi, wr], 1))):
            high, low = split(w)
            out[2 * k] = high
            out[2 * k + 1] = low
        width = 32 if adj else 16
        sides = []
        for side in range(2):
            first = 32 if side else 32 - width
            rr, ri = wr[first : first + width, :32], wi[first : first + width, :32]
            both = jnp.concatenate([jnp.concatenate([rr, ri], 1), jnp.concatenate([-ri, rr], 1)], 0)
            high, low = split(both)
            one = jnp.concatenate([high, high, low], 0)
            none = jnp.zeros_like(one)
            sides.append(jnp.concatenate([none, one] if side else [one, none], 1))
        (cxc if adj else cxw)[...] = jnp.concatenate(sides, 0)

    zero = jnp.zeros((32, HX), BF16)
    for k in range(4):
        for ref in (xh, xl):
            ref[k, 0:32] = zero
            ref[k, 352:384] = zero
            ref[k, 384:416] = zero
    for k in range(2):
        t1o[k, 0:16] = jnp.zeros((16, WIDE), F32)
        t1o[k, 336:352] = jnp.zeros((16, WIDE), F32)

    def rows(n, carry):
        at = pl.ds(pl.multiple_of(n * 32, 32), 32)
        to = pl.ds(pl.multiple_of(n * 32 + 32, 32), 32)
        c, s = cos_sin(ph[0, at])
        t0[0, at] = c
        t0[1, at] = s
        r, i = inc[0, at], inc[1, at]
        for k, v in enumerate((r * c - i * s, r * s + i * c, cot[0, at], cot[1, at])):
            high, low = split(v)
            xh[k, to] = high
            xl[k, to] = low
        mid = pl.ds(pl.multiple_of(n * 32 + 16, 16), 32)
        left, right = jnp.zeros((32, 16), F32), jnp.zeros((32, WIDE - HX - 16), F32)
        for k, v in enumerate(cos_sin(ph[1, at])):
            t1o[k, mid] = jnp.concatenate([left, v, right], 1)
        return carry

    lax.fori_loop(0, HY // 32, rows, 0)

    for field, band in ((0, af), (1, aa)):
        for b in range(3):
            win = slice(BLOCK * b, BLOCK * b + SPAN)
            got = [
                dot(band[...], jnp.concatenate([xh[k, win], xl[k, win], xh[k, win]], 0))
                for k in (2 * field, 2 * field + 1)
            ]
            n = min(BLOCK, EY - BLOCK * b)
            to = slice(BLOCK * b, BLOCK * b + n)
            m[2 * field, to] = got[0][:n] - got[1][BLOCK : BLOCK + n]
            m[2 * field + 1, to] = got[1][:n] + got[0][BLOCK : BLOCK + n]


def seam_kernel(m_in, top, bottom, ph, cy, m, right, left):
    none = jnp.zeros((16, HX), F32)
    for side, rim in enumerate((top, bottom)):
        for field in range(2):
            got = []
            for part in range(2):
                if field:
                    x = rim[32 + 32 * part : 64 + 32 * part]
                else:
                    x = rim[16 * part : 16 * part + 16]
                    x = jnp.concatenate([x, none] if side else [none, x], 0)
                high, low = split(x)
                got.append(dot(cy[2 * field + side], jnp.concatenate([high, low, high], 0)))
            at = slice(EY - 32, EY) if side else slice(0, 32)
            m[2 * field, at] = m_in[2 * field, at] + got[0][:32] - got[1][32:]
            m[2 * field + 1, at] = m_in[2 * field + 1, at] + got[1][:32] + got[0][32:]
    for out, one, two in ((right, HX - 16, HX - 32), (left, 0, 0)):
        for a, b in ((0, 16), (16, 336), (336, 352)):
            src = m if b - a < 32 else m
            if a == 0:
                p = top[96:112, one : one + 16]
            elif a == 16:
                p = ph[1, :, one : one + 16]
            else:
                p = bottom[96:112, one : one + 16]
            out[a:b] = jnp.concatenate(
                [
                    src[0, a:b, one : one + 16],
                    src[1, a:b, one : one + 16],
                    src[2, a:b, two : two + 32],
                    src[3, a:b, two : two + 32],
                    p,
                    jnp.zeros((b - a, 16), F32),
                ],
                1,
            )


def across(high, low, w, k, win, at=slice(0, EY)):
    n = win.stop - win.start
    return (
        dot(high[k, at, win], w[0, :n])
        + dot(low[k, at, win], w[0, :n])
        + dot(high[k, at, win], w[1, :n])
        + dot(high[k + 1, at, win], w[2, :n])
        + dot(low[k + 1, at, win], w[2, :n])
        + dot(high[k + 1, at, win], w[3, :n])
    )


def window(t):
    return slice(BLOCK * t, min(BLOCK * t + SPAN, WIDE))


def down_blocks(band, high, low, store):
    for b in range(3):
        win = slice(BLOCK * b, BLOCK * b + SPAN)
        got = [dot(band[...], jnp.concatenate([h[win], l[win], h[win]], 0)) for h, l in zip(high, low)]
        store(slice(BLOCK * b, min(BLOCK * b + BLOCK, HY)), got)


def inner_kernel(m, t1_in, top, bottom, aa, wf, wa, fs, gs, gz, pg, eh, el, gh, gl, yh, yl, prod, t1o):
    t1o[...] = t1_in[...]
    for at, rim in ((slice(0, 16), top), (slice(336, 352), bottom)):
        left, right = jnp.zeros((16, 16), F32), jnp.zeros((16, WIDE - HX - 16), F32)
        for k, v in enumerate(cos_sin(rim[96:112])):
            t1o[k, at] = jnp.concatenate([left, v, right], 1)

    def rows(n, carry):
        at = pl.ds(pl.multiple_of(n * 32, 32), 32)
        left, right = jnp.zeros((32, 32), F32), jnp.zeros((32, WIDE - HX - 32), F32)
        for k in range(4):
            high, low = split(jnp.concatenate([left, m[k, at], right], 1))
            eh[k, at] = high
            el[k, at] = low
        return carry

    lax.fori_loop(0, EY // 32, rows, 0)

    lane = lax.broadcasted_iota(jnp.int32, (1, BLOCK), 1)
    inside = slice(RIM, RIM + HY)
    for k in range(2):
        for ref in (gh, gl):
            ref[k, 352:384] = jnp.zeros((32, WIDE), BF16)
            ref[k, 384:416] = jnp.zeros((32, WIDE), BF16)
    for t in range(4):
        at = slice(BLOCK * t, BLOCK * t + BLOCK)
        f = across(eh, el, wf, 0, window(t), inside)
        grad = across(eh, el, wa, 2, window(t))
        c, s = t1o[0, :, at], t1o[1, :, at]
        fr, fi = f[:, :BLOCK], f[:, BLOCK:]
        gr, gi = grad[:, :BLOCK], grad[:, BLOCK:]
        if t in (0, 3):
            to = slice(0, 64) if t == 0 else slice(64, 128)
            gs[:, to] = jnp.concatenate([gr[:, :32], gi[:, :32]], 1)
            fs[:, to] = jnp.concatenate([fr[:, :32], fi[:, :32]], 1)
        r, i = gr * c + gi * s, gi * c - gr * s
        if t == 0:
            keep = lane >= 32
            r, i = jnp.where(keep, r, 0.0), jnp.where(keep, i, 0.0)
        if t == 3:
            r, i = jnp.zeros_like(r), jnp.zeros_like(i)
        prod[:, at] = i[inside] * fr - r[inside] * fi
        for k, v in enumerate((r, i)):
            high, low = split(v)
            gh[k, 0:EY, at] = high
            gl[k, 0:EY, at] = low
    pg[...] = prod[:, RIM : RIM + HX]

    def keep_rows(at, got):
        n = at.stop - at.start
        yr = got[0][:n] - got[1][BLOCK : BLOCK + n]
        yi = got[1][:n] + got[0][BLOCK : BLOCK + n]
        for k, v in enumerate((yr, yi)):
            high, low = split(v)
            yh[k, at] = high
            yl[k, at] = low

    down_blocks(aa, [gh.at[0], gh.at[1]], [gl.at[0], gl.at[1]], keep_rows)
    for t in range(3):
        z = across(yh, yl, wa, 0, window(t), slice(0, HY))
        at = slice(BLOCK * t, BLOCK * t + BLOCK)
        gz[0, :, at] = z[:, :BLOCK]
        gz[1, :, at] = z[:, BLOCK:]


def high_low_high(x):
    high, low = split(x)
    return jnp.concatenate([high, low, high], 1)


def swap(x, lane):
    return jnp.where((lane & 32) == 0, pltpu.roll(x, 96, 1), pltpu.roll(x, 32, 1))


def final_kernel(hl, hr, right, left, fs, gs, gz, pg, t0, inc, aa, cxw, cxc, phase, probe, sh, sl):
    lane = lax.broadcasted_iota(jnp.int32, (1, BLOCK), 1)
    real = (lane & 32) == 0
    f = fs[...] + dot(
        jnp.concatenate([high_low_high(hl[16:336, 0:32]), high_low_high(hr[16:336, 0:32])], 1), cxw[...]
    )
    g = gs[...] + dot(jnp.concatenate([high_low_high(hl[:, 32:96]), high_low_high(hr[:, 32:96])], 1), cxc[...])
    near = jnp.concatenate([hl[:, 96:112], left[:, 96:112]], 1)
    far = jnp.concatenate([right[:, 96:112], hr[:, 96:112]], 1)
    c, s = cos_sin(jnp.concatenate([near, near, far, far], 1))
    g = g * c + swap(g, lane) * jnp.where(real, s, -s)
    both = g[16:336] * jnp.where(real, -1.0, 1.0) * swap(f, lane)
    edge = both + swap(both, lane)
    high, low = split(g)
    sh[0:EY] = high
    sl[0:EY] = low
    sh[EY:PAD] = jnp.zeros((PAD - EY, BLOCK), BF16)
    sl[EY:PAD] = jnp.zeros((PAD - EY, BLOCK), BF16)

    fix = [None, None]

    def across_strip(at, got):
        n = at.stop - at.start
        a, b = got[0][:n], got[0][BLOCK : BLOCK + n]
        y = a + swap(b, lane) * jnp.where(real, -1.0, 1.0)
        x = jnp.concatenate([high_low_high(y[:, :64]), high_low_high(y[:, 64:])], 1)
        z = dot(x, cxc[...])
        for t in range(3):
            cols = slice(BLOCK * t, BLOCK * t + BLOCK)
            zr, zi = gz[0, at, cols], gz[1, at, cols]
            e = pg[at, cols]
            if t == 0:
                on = lane < 32
                zr = zr + jnp.where(on, z, 0.0)
                zi = zi + jnp.where(on, pltpu.roll(z, 96, 1), 0.0)
                e = jnp.where(lane < 16, pltpu.roll(edge[at], BLOCK - 16, 1), e)
            if t == 2:
                on = lane >= 96
                zr = zr + jnp.where(on, pltpu.roll(z, 32, 1), 0.0)
                zi = zi + jnp.where(on, z, 0.0)
                e = jnp.where(lane >= 112, pltpu.roll(edge[at], 48, 1), e)
            c, s = t0[0, at, cols], t0[1, at, cols]
            pr, pi = zr * c + zi * s, zi * c - zr * s
            probe[0, at, cols] = pr
            probe[1, at, cols] = pi
            phase[0, at, cols] = pi * inc[0, at, cols] - pr * inc[1, at, cols]
            phase[1, at, cols] = e

    down_blocks(aa, [sh], [sl], across_strip)


def on_device(incident, phases, cotangent, propagator):
    sds = jax.ShapeDtypeStruct
    params = pltpu.CompilerParams(vmem_limit_bytes=48 << 20)
    up, down = pl.pallas_call(
        edge_kernel,
        out_shape=(sds((112, HX), F32),) * 2,
        in_specs=[pl.BlockSpec(memory_space=pl.ANY)] * 3,
        out_specs=(VM, VM),
        scratch_shapes=[
            pltpu.VMEM((2, 2, RIM, HX), F32),
            pltpu.VMEM((2, RIM, HX), F32),
            pltpu.SemaphoreType.DMA((10,)),
        ],
        compiler_params=params,
        name="edges",
    )(incident, phases, cotangent)
    ty, tx = lax.axis_size("ty"), lax.axis_size("tx")
    top = lax.ppermute(up, "ty", [(i, (i + 1) % ty) for i in range(ty)])
    bottom = lax.ppermute(down, "ty", [((i + 1) % ty, i) for i in range(ty)])

    taps = jnp.pad(jnp.concatenate([propagator, propagator[:, ::-1]], 0), ((0, 4), (0, 256 - TAPS)))
    m, t0, t1o, aa, wf, wa, cy, cxw, cxc = pl.pallas_call(
        local_kernel,
        out_shape=(
            sds((4, EY, HX), F32),
            sds((2, HY, HX), F32),
            sds((2, EY, WIDE), F32),
            sds((2 * BLOCK, 3 * SPAN), BF16),
            sds((4, SPAN, 2 * BLOCK), BF16),
            sds((4, SPAN, 2 * BLOCK), BF16),
            sds((4, 64, 96), BF16),
            sds((192, BLOCK), BF16),
            sds((384, BLOCK), BF16),
        ),
        in_specs=[VM] * 4,
        out_specs=(VM,) * 9,
        scratch_shapes=[
            pltpu.VMEM((4, PAD, HX), BF16),
            pltpu.VMEM((4, PAD, HX), BF16),
            pltpu.VMEM((2 * BLOCK, 3 * SPAN), BF16),
        ],
        compiler_params=params,
        name="local",
    )(taps, incident, phases, cotangent)

    m, right, left = pl.pallas_call(
        seam_kernel,
        out_shape=(sds((4, EY, HX), F32), sds((EY, BLOCK), F32), sds((EY, BLOCK), F32)),
        in_specs=[VM] * 5,
        out_specs=(VM,) * 3,
        input_output_aliases={0: 0},
        compiler_params=params,
        name="seam",
    )(m, top, bottom, phases, cy)
    hl = lax.ppermute(right, "tx", [(i, (i + 1) % tx) for i in range(tx)])
    hr = lax.ppermute(left, "tx", [((i + 1) % tx, i) for i in range(tx)])

    fs, gs, gz, pg = pl.pallas_call(
        inner_kernel,
        out_shape=(
            sds((HY, BLOCK), F32),
            sds((EY, BLOCK), F32),
            sds((2, HY, HX), F32),
            sds((HY, HX), F32),
        ),
        in_specs=[VM] * 7,
        out_specs=(VM,) * 4,
        scratch_shapes=[
            pltpu.VMEM((4, EY, WIDE), BF16),
            pltpu.VMEM((4, EY, WIDE), BF16),
            pltpu.VMEM((2, PAD, WIDE), BF16),
            pltpu.VMEM((2, PAD, WIDE), BF16),
            pltpu.VMEM((2, HY, WIDE), BF16),
            pltpu.VMEM((2, HY, WIDE), BF16),
            pltpu.VMEM((HY, WIDE), F32),
            pltpu.VMEM((2, EY, WIDE), F32),
        ],
        compiler_params=params,
        name="inner",
    )(m, t1o, top, bottom, aa, wf, wa)

    return pl.pallas_call(
        final_kernel,
        out_shape=(sds((2, HY, HX), F32), sds((2, HY, HX), F32)),
        in_specs=[VM] * 13,
        scratch_shapes=[pltpu.VMEM((PAD, BLOCK), BF16), pltpu.VMEM((PAD, BLOCK), BF16)],
        compiler_params=params,
        name="final",
    )(hl, hr, right, left, fs, gs, gz, pg, t0, incident, aa, cxw, cxc)


def solution(mesh):
    placed = (P(None, "ty", "tx"), P(None, "ty", "tx"), P(None, "ty", "tx"), P())
    return jax.shard_map(
        on_device,
        mesh=mesh,
        in_specs=placed,
        out_specs=(P(None, "ty", "tx"), P(None, "ty", "tx")),
        check_vma=False,
    )
```
